32 devices in a mesh: row: 4 (over y, core), col: 8 (over z, x).
Axes of the slice: x: 2, y: 2, z: 4, core: 2. Of those that a mesh axis runs over, the one named last changes fastest.
Arguments:
- integrals: bfloat16 [4, 8, 32, 512, 512], P('row', 'col'), may hold values from -0.0625 to 0.0625
- tile_count: int32 [4, 8], P('row', 'col'), may hold values from 1 to 32, as said below
- tile_list: int32 [4, 8, 32], P('row', 'col'), may hold values from 0 to 31, as said below
- amplitudes: bfloat16 [32, 512, 1024], P('col', 'row'), may hold values from -6 to 6
- pair_energy: float32 [16384], P(('row', 'col')), may hold values from 1 to 4
- occ_energy: float32 [32], replicated, may hold values from -1.5 to -0.25
- partner: int32 [16384], P(('row', 'col')), may hold values from 0 to 16383, as said below
Outputs:
- amp_update: float32 [16384, 1024], P(('row', 'col'))
The draws below stay inside these ranges and needn't reach their ends.
Inputs may be any that keep to these rules, and one draw needn't show every extreme that they name: `tile_count`: some grid cell holds exactly 32 live tiles. `tile_list`: each grid cell's list is a permutation of 0 to 31; only its first tile_count entries name live tiles. partner is an involution. Numbering the rows in consecutive blocks of 512, the rows of one block have their partners among the 8 blocks of the same aligned group of 4096 rows, exactly 64 of them in each of these blocks.
All inputs are finite; a program needn't handle non-finite values.
Results may differ from the reference program's by a relative error of at most 0.0003.
Values may be sent and summed in bfloat16 or wider, within the bound.
A program may use at most 128 MiB of HBM per device.

```python
import math
import jax
import jax.numpy as jnp
from jax import lax

TILE = 512
NO = 32
BC = 4
OCC = 1024
NBLK = 32
BR = 8
CAP = 32
NPAIRS = 16384
ROWS = 512
PEER = 64
N_ROW = 4
N_COL = 8


def shuffle_cap(subkey):
    return jax.random.permutation(subkey, CAP).astype(jnp.int32)


def shuffle_rows(subkey):
    return jax.random.permutation(subkey, ROWS).astype(jnp.int32)


def draw_tile_count(key, part):
    counts = jax.random.randint(key, (N_ROW * N_COL,), 1, CAP + 1).astype(jnp.int32)
    chosen = jax.random.randint(jax.random.fold_in(key, 7), (), 0, N_ROW * N_COL)
    counts = jnp.where(jnp.arange(N_ROW * N_COL) == chosen, CAP, counts)
    return counts.reshape(N_ROW, N_COL).astype(jnp.int32)


def draw_tile_list(key, part):
    subkeys = jax.random.split(jax.random.fold_in(key, 11), N_ROW * N_COL)
    orders = jax.vmap(shuffle_cap)(subkeys)
    return orders.reshape(N_ROW, N_COL, CAP).astype(jnp.int32)


def draw_partner(key, part):
    subkeys = jax.random.split(jax.random.fold_in(key, 13), N_ROW * N_COL)
    orders = jax.vmap(shuffle_rows)(subkeys).reshape(N_ROW, N_COL, ROWS)
    inverse = jnp.argsort(orders, axis=2).astype(jnp.int32)
    target = inverse // PEER
    within = inverse % PEER
    grid_row = jnp.arange(N_ROW, dtype=jnp.int32)[:, None, None]
    grid_col = jnp.arange(N_COL, dtype=jnp.int32)[None, :, None]
    local_row = orders[grid_row, target, grid_col * PEER + within]
    result = (grid_row * N_COL + target) * ROWS + local_row
    return result.reshape(N_ROW * N_COL * ROWS).astype(jnp.int32)


def block_levels(stream_key, dims, cuts, least, largest):
    gain, own = 1.0, jax.random.fold_in(stream_key, 6)
    for axis_at, blocks in cuts:
        draws = jnp.exp(jax.random.uniform(jax.random.fold_in(own, axis_at), (blocks,), jnp.float32, least / len(cuts), largest / len(cuts)))
        gain = gain * jnp.repeat(draws, dims[axis_at] // blocks).reshape([-1 if axis == axis_at else 1 for axis in range(len(dims))])
    return gain


def noise(rng, dims, spread, most, cuts=(), held_as=jnp.bfloat16):
    drawn = spread * jax.random.normal(rng, dims, jnp.float32)
    if cuts:
        drawn = drawn * block_levels(rng, dims, cuts, -0.22, 0.18)
    return jnp.clip(drawn, -most, most).astype(held_as)


def setup_inputs(seed: int = 0) -> dict:
    key_list = jax.random.split(jax.random.key(seed), 8)
    return {
        "integrals": noise(key_list[0], (N_ROW, N_COL, CAP, TILE, TILE), (NBLK * TILE // 2) ** -0.5, 0.0625, ((0, 4), (1, 8))),
        "tile_count": draw_tile_count(jax.random.fold_in(key_list[7], 71), 0),
        "tile_list": draw_tile_list(jax.random.fold_in(key_list[7], 71), 0),
        "amplitudes": noise(key_list[3], (NBLK, TILE, OCC), 1.0, 6.0, ((0, 8), (1, 4))),
        "pair_energy": jnp.clip(jnp.exp(math.log(4.0) - 1.3862944 * jax.random.uniform(key_list[4], (NPAIRS,), jnp.float32) ** block_levels(key_list[4], (NPAIRS,), ((0, 32),), -0.2, 0.2)), 1.0, 4.0),
        "occ_energy": jnp.clip(jax.random.uniform(key_list[5], (NO,), jnp.float32, -1.5, -0.25), -1.5, -0.25),
        "partner": draw_partner(jax.random.fold_in(key_list[7], 71), 0),
    }


def reference(integrals, tile_count, tile_list, amplitudes, pair_energy, occ_energy, partner):
    residual = jnp.zeros((NBLK, TILE, OCC), jnp.float32)

    def per_device(device, running):
        grid_row = (device // N_COL).astype(jnp.int32)
        grid_col = (device % N_COL).astype(jnp.int32)
        count_here = tile_count[grid_row, grid_col]

        def per_slot(slot, inner):
            position = tile_list[grid_row, grid_col, slot]
            block_row = grid_row * BR + position // BC
            block_col = grid_col * BC + position % BC
            product = jnp.dot(integrals[grid_row, grid_col, slot], amplitudes[block_col], preferred_element_type=jnp.float32)
            current = lax.dynamic_index_in_dim(inner, block_row, 0, keepdims=False)
            return lax.dynamic_update_index_in_dim(inner, current + product, block_row, 0)

        return lax.fori_loop(0, count_here, per_slot, running)

    residual = lax.fori_loop(0, N_ROW * N_COL, per_device, residual)
    flat_rows = residual.reshape(NPAIRS, OCC)
    mirrored = jnp.take(flat_rows, partner, axis=0).reshape(NPAIRS, NO, NO)
    mirrored = jnp.swapaxes(mirrored, 1, 2).reshape(NPAIRS, OCC)
    denominator = pair_energy[:, None] - (occ_energy[:, None] + occ_energy[None, :]).reshape(1, OCC)
    return (flat_rows + mirrored) / denominator
```

```python
import functools

import jax
import jax.numpy as jnp
from jax import lax
from jax.experimental import pallas as pl
from jax.experimental.pallas import tpu as pltpu
from jax.sharding import PartitionSpec as P

MESH = pl.DeviceIdType.MESH
F32, BF16, I32, I16 = jnp.float32, jnp.bfloat16, jnp.int32, jnp.int16
LEVELS = 32767.0


def iota(shape, axis):
    return lax.broadcasted_iota(I32, shape, axis)


def row_places(partner, me, n):
    rows = partner.shape[0]
    half = rows // n // 2
    own = (n + 1) * half
    local = partner % (n * rows)
    block, within = local // rows, local % rows
    index = jnp.arange(rows, dtype=I32)
    key = jnp.where(block < me, within, index)
    before = (block[None, :] == block[:, None]) & (key[None, :] < key[:, None])
    rank = jnp.sum(before.astype(I32), axis=1)
    shift = (block - me + n) % n
    owned = jnp.where(me < block, rank < half, rank >= half)
    step = (shift - 1) * half + rank % half
    place = jnp.where(block == me, rank, jnp.where(owned, 2 * half + step, own + step))
    found = jnp.sum(jnp.where(index[None, :] == within[:, None], place[None, :], 0), axis=1)
    mirror = jnp.where(block == me, rows + found, -1)
    return place, mirror


def sort_kernel(n, half, occ, slot_ref, live_ref, tile_ref, place_ref, u_ref, w_ref, swap_ref):
    c, i = pl.program_id(0), pl.program_id(1)
    rows = place_ref.shape[2]
    tile = tile_ref.shape[3]
    own = (n + 1) * half
    live = live_ref[i * pl.num_programs(0) + c]

    @pl.when((c == 0) & (i == 0))
    def _():
        total = swap_ref.shape[0]
        chunk = 128

        @pl.loop(0, total // chunk)
        def _(k):
            x = iota((chunk, total), 0) + k * chunk
            y = iota((chunk, total), 1)
            hit = x == (y % occ) * occ + y // occ
            swap_ref[pl.ds(pl.multiple_of(k * chunk, chunk), chunk), :] = hit.astype(F32).astype(BF16)

    for j in range(tile // rows):
        o = i * (tile // rows) + j
        place = place_ref[o]
        hit = (iota((rows, rows), 0) == place) & (live > 0)
        one_hot = hit.astype(F32).astype(BF16)
        got = jnp.dot(one_hot, tile_ref[0, 0, 0, j * rows : (j + 1) * rows, :], preferred_element_type=F32)
        u_ref[o] = got[:own].astype(BF16)
        for d in range(1, n):
            a = lax.rem(o + d, n)
            start = (n - d - 1) * half
            w_ref[a, start : start + half, :] = got[own + (d - 1) * half : own + d * half].astype(BF16)


def reduce_kernel(
    n, half, u_hbm, w_hbm, t_hbm, swap_hbm, z_ref,
    ubuf, wbuf, tbuf, t2buf, swap, sbuf, qsend, ssend, qrecv, srecv, fbuf,
    usem, wsem, tsem, psem, qs, qr, ss, sr, xs, xr,
):
    me = lax.axis_index("col")
    depth, width = tbuf.shape
    own = (n + 1) * half
    chunks = n + 1

    load_t = pltpu.make_async_copy(t_hbm, tbuf, tsem)
    load_p = pltpu.make_async_copy(swap_hbm, swap, psem)
    load_t.start()
    load_p.start()

    def load(a):
        return (
            pltpu.make_async_copy(u_hbm.at[a], ubuf.at[a], usem.at[a]),
            pltpu.make_async_copy(w_hbm.at[a], wbuf.at[a], wsem.at[a]),
        )

    for step in range(n):
        for copy in load(lax.rem(me + 1 + step, n)):
            copy.start()

    barrier = pltpu.get_barrier_semaphore()
    for d in range(1, n):
        pl.semaphore_signal(barrier, inc=1, device_id={"col": lax.rem(me + d, n)}, device_id_type=MESH)
    pl.semaphore_wait(barrier, n - 1)

    load_t.wait()
    load_p.wait()
    high = 256

    @pl.loop(0, depth // high)
    def _(k):
        at = pl.ds(pl.multiple_of(k * high, high), high)
        for c in range(0, width, 256):
            t2buf[at, c : c + 256] = jnp.dot(tbuf[at, :], swap[:, c : c + 256], preferred_element_type=F32).astype(BF16)

    def product(a, out):
        for copy in load(a):
            copy.wait()

        @pl.loop(0, width // 256)
        def _(c):
            at = pl.ds(pl.multiple_of(c * 256, 256), 256)
            first = jnp.dot(ubuf[a], tbuf[:, at], preferred_element_type=F32)
            second = jnp.dot(wbuf[a], t2buf[:, at], preferred_element_type=F32)
            out[0 : 2 * half, at] = first[: 2 * half]
            out[2 * half : own, at] = first[2 * half :] + second

    def q_copy(a, source):
        return (
            pltpu.make_async_remote_copy(
                src_ref=qsend.at[a], dst_ref=qrecv.at[source], send_sem=qs.at[a], recv_sem=qr.at[source],
                device_id={"col": a}, device_id_type=MESH,
            ),
            pltpu.make_async_remote_copy(
                src_ref=ssend.at[a], dst_ref=srecv.at[source], send_sem=ss.at[a], recv_sem=sr.at[source],
                device_id={"col": a}, device_id_type=MESH,
            ),
        )

    diagonal = iota((half, 128), 0) == iota((half, 128), 1)

    @pl.loop(0, n - 1)
    def _(step):
        a = lax.rem(me + 1 + step, n)
        product(a, sbuf)
        for k in range(chunks):
            part = sbuf[k * half : (k + 1) * half, :]
            most = jnp.max(jnp.abs(part), axis=1, keepdims=True)
            scale = most * (1.0 / LEVELS)
            inverse = jnp.where(most > 1e-30, LEVELS / jnp.maximum(most, 1e-30), 0.0)
            level = jnp.round(part * inverse)
            qsend[a, k] = level.astype(I32).astype(I16)
            ssend[a, k : k + 1, :] = jnp.sum(jnp.where(diagonal, scale, 0.0), axis=0, keepdims=True)
        for copy in q_copy(a, me):
            copy.start()

    product(me, z_ref)

    @pl.loop(1, n)
    def _(d):
        source = lax.rem(me + n - d, n)
        for copy in q_copy(source, source):
            copy.wait_recv()
        for k in range(chunks):
            scale = jnp.sum(jnp.where(diagonal, srecv[source, k : k + 1, :], 0.0), axis=1, keepdims=True)
            z_ref[k * half : (k + 1) * half, :] += qrecv[source, k].astype(I32).astype(F32) * scale

    def x_copy(d):
        return pltpu.make_async_remote_copy(
            src_ref=z_ref.at[pl.ds((d + 1) * half, half)], dst_ref=fbuf.at[pl.ds((n - d - 1) * half, half)],
            send_sem=xs.at[d], recv_sem=xr.at[n - d],
            device_id={"col": lax.rem(me + d, n)}, device_id_type=MESH,
        )

    for d in range(1, n):
        x_copy(d).start()
    for d in range(1, n):
        x_copy(d).wait_recv()
    z_ref[own:, :] = fbuf[...]
    for d in range(1, n):
        x_copy(d).wait_send()

    @pl.loop(1, n)
    def _(d):
        for copy in q_copy(lax.rem(me + d, n), me):
            copy.wait_send()


def final_kernel(half, own, z_ref, swap_ref, place_ref, mirror_ref, pair_ref, occ_ref, out_ref, pieces):
    rows, width = z_ref.shape

    @pl.when(pl.program_id(0) == 0)
    def _():
        rest = z_ref[...]
        for p in range(3):
            piece = rest.astype(BF16)
            pieces[p] = piece
            rest = rest - piece.astype(F32)

    chunk = out_ref.shape[1]
    at = pl.ds(pl.multiple_of(pl.program_id(0) * chunk, chunk), chunk)
    place, mirror = place_ref[...], mirror_ref[...]

    def hot(count, first):
        number = iota((rows, count), 1) + first
        return ((number == place) | (number == mirror)).astype(F32).astype(BF16)

    hot_own, hot_far, hot_self = hot(own, 0), hot(rows - own, own), hot(2 * half, rows)
    mixer = swap_ref[...]
    total = None
    for p in (2, 1, 0):
        far = jnp.dot(pieces[p, own:, :], mixer, preferred_element_type=F32).astype(BF16)
        near = jnp.dot(pieces[p, : 2 * half, :], mixer, preferred_element_type=F32).astype(BF16)
        term = jnp.dot(hot_own, pieces[p, :own, at], preferred_element_type=F32)
        mine = jnp.dot(hot_self, near, preferred_element_type=F32)
        other = jnp.dot(hot_far, far, preferred_element_type=F32)
        term = term + (mine + other)
        total = term if total is None else total + term
    out_ref[...] = total / (pair_ref[...] - occ_ref[...])


def body(integrals, tile_count, tile_list, amplitudes, pair_energy, occ_energy, partner):
    n = lax.axis_size("col")
    me = lax.axis_index("col")
    rows = partner.shape[0]
    half = rows // n // 2
    own = (n + 1) * half
    slots, tile = integrals.shape[2], integrals.shape[3]
    bc, _, width = amplitudes.shape
    br = slots // bc
    occ = occ_energy.shape[0]
    depth = bc * tile

    place, mirror = row_places(partner, me, n)
    places = lax.all_gather(place, "col", axis=0, tiled=True).reshape(n, 1, rows)
    gathered = lax.all_gather(amplitudes, "row", axis=1, tiled=True).reshape(depth, width)

    number = jnp.arange(slots, dtype=I32)
    slot = jnp.sum(jnp.where(tile_list[0, 0][None, :] == number[:, None], number[None, :], 0), axis=1)
    live = (slot < tile_count[0, 0]).astype(I32)

    u, w, swap = pl.pallas_call(
        functools.partial(sort_kernel, n, half, occ),
        grid_spec=pltpu.PrefetchScalarGridSpec(
            num_scalar_prefetch=2,
            grid=(bc, br),
            in_specs=[
                pl.BlockSpec((1, 1, 1, tile, tile), lambda c, i, s, l: (0, 0, s[i * bc + c], 0, 0)),
                pl.BlockSpec((n, 1, rows), lambda c, i, s, l: (0, 0, 0)),
            ],
            out_specs=[
                pl.BlockSpec((n, own, tile), lambda c, i, s, l: (0, 0, c)),
                pl.BlockSpec((n, rows - own, tile), lambda c, i, s, l: (0, 0, c)),
                pl.BlockSpec((width, width), lambda c, i, s, l: (0, 0)),
            ],
        ),
        out_shape=[
            jax.ShapeDtypeStruct((n, own, depth), BF16),
            jax.ShapeDtypeStruct((n, rows - own, depth), BF16),
            jax.ShapeDtypeStruct((width, width), BF16),
        ],
        compiler_params=pltpu.CompilerParams(vmem_limit_bytes=40 * 1024 * 1024),
        cost_estimate=pl.CostEstimate(
            flops=2 * slots * rows * tile * tile, bytes_accessed=4 * slots * tile * tile, transcendentals=0
        ),
        name="sort_rows",
    )(slot, live, integrals, places)

    anywhere = pl.BlockSpec(memory_space=pl.ANY)
    scale_rows = -(-(n + 1) // 8) * 8
    dma = pltpu.SemaphoreType.DMA
    z = pl.pallas_call(
        functools.partial(reduce_kernel, n, half),
        out_shape=jax.ShapeDtypeStruct((rows, width), F32),
        in_specs=[anywhere] * 4,
        out_specs=pl.BlockSpec(memory_space=pltpu.VMEM),
        scratch_shapes=[
            pltpu.VMEM((n, own, depth), BF16),
            pltpu.VMEM((n, rows - own, depth), BF16),
            pltpu.VMEM((depth, width), BF16),
            pltpu.VMEM((depth, width), BF16),
            pltpu.VMEM((width, width), BF16),
            pltpu.VMEM((own, width), F32),
            pltpu.VMEM((n, n + 1, half, width), I16),
            pltpu.VMEM((n, scale_rows, 128), F32),
            pltpu.VMEM((n, n + 1, half, width), I16),
            pltpu.VMEM((n, scale_rows, 128), F32),
            pltpu.VMEM((rows - own, width), F32),
            dma((n,)), dma((n,)), dma, dma,
            dma((n,)), dma((n,)), dma((n,)), dma((n,)), dma((n,)), dma((n,)),
        ],
        compiler_params=pltpu.CompilerParams(
            collective_id=0, has_side_effects=True, vmem_limit_bytes=63 * 1024 * 1024
        ),
        name="reduce_pairs",
    )(u, w, gathered, swap)

    chunk = 256
    whole = lambda k: (0, 0)
    return pl.pallas_call(
        functools.partial(final_kernel, half, own),
        grid=(width // chunk,),
        in_specs=[
            pl.BlockSpec((rows, width), whole),
            pl.BlockSpec((width, chunk), lambda k: (0, k)),
            pl.BlockSpec((rows, 1), whole),
            pl.BlockSpec((rows, 1), whole),
            pl.BlockSpec((rows, 1), whole),
            pl.BlockSpec((1, chunk), lambda k: (0, k)),
        ],
        out_specs=pl.BlockSpec((rows, chunk), lambda k: (0, k)),
        out_shape=jax.ShapeDtypeStruct((rows, width), F32),
        scratch_shapes=[pltpu.VMEM((3, rows, width), BF16)],
        compiler_params=pltpu.CompilerParams(vmem_limit_bytes=40 * 1024 * 1024),
        name="finish_rows",
    )(
        z, swap, place[:, None], mirror[:, None], pair_energy[:, None],
        (occ_energy[:, None] + occ_energy[None, :]).reshape(1, width),
    )


def solution(mesh):
    return jax.shard_map(
        body,
        mesh=mesh,
        in_specs=(
            P("row", "col", None, None, None),
            P("row", "col"),
            P("row", "col", None),
            P("col", "row", None),
            P(("row", "col")),
            P(),
            P(("row", "col")),
        ),
        out_specs=P(("row", "col"), None),
        check_vma=False,
    )
```

```python
import functools

import jax
import jax.numpy as jnp
from jax import lax
from jax.experimental import pallas as pl
from jax.experimental.pallas import tpu as pltpu
from jax.sharding import PartitionSpec as P

MESH = pl.DeviceIdType.MESH
F32, BF16, I32, I16 = jnp.float32, jnp.bfloat16, jnp.int32, jnp.int16
LEVELS = 32767.0


def iota(shape, axis):
    return lax.broadcasted_iota(I32, shape, axis)


def row_places(partner, me, n):
    rows = partner.shape[0]
    half = rows // n // 2
    own = (n + 1) * half
    local = partner % (n * rows)
    block, within = local // rows, local % rows
    index = jnp.arange(rows, dtype=I32)
    key = jnp.where(block < me, within, index)
    before = (block[None, :] == block[:, None]) & (key[None, :] < key[:, None])
    rank = jnp.sum(before.astype(I32), axis=1)
    shift = (block - me + n) % n
    owned = jnp.where(me < block, rank < half, rank >= half)
    step = (shift - 1) * half + rank % half
    place = jnp.where(block == me, rank, jnp.where(owned, 2 * half + step, own + step))
    found = jnp.sum(jnp.where(index[None, :] == within[:, None], place[None, :], 0), axis=1)
    mirror = jnp.where(block == me, rows + found, -1)
    return place, mirror


def gather_kernel(n, mine_ref, all_ref, landed, send_sem, recv_sem):
    me = lax.axis_index("col")
    barrier = pltpu.get_barrier_semaphore()
    for d in range(1, n):
        pl.semaphore_signal(barrier, inc=1, device_id={"col": lax.rem(me + d, n)}, device_id_type=MESH)
    pl.semaphore_wait(barrier, n - 1)

    def copy(d):
        return pltpu.make_async_remote_copy(
            src_ref=mine_ref, dst_ref=landed.at[d], send_sem=send_sem.at[d], recv_sem=recv_sem.at[d],
            device_id={"col": lax.rem(me + d, n)}, device_id_type=MESH,
        )

    for d in range(1, n):
        copy(d).start()
    all_ref[me] = mine_ref[...]
    for d in range(1, n):
        copy(d).wait_recv()
        all_ref[lax.rem(me + n - d, n)] = landed[d]
    for d in range(1, n):
        copy(d).wait_send()


def sort_kernel(n, half, occ, bc, slot_ref, live_ref, *refs):
    tiles, (place_ref, u_ref, w_ref, swap_ref) = refs[:bc], refs[bc:]
    i = pl.program_id(0)
    rows = place_ref.shape[2]
    tile = tiles[0].shape[3]
    own = (n + 1) * half

    total = swap_ref.shape[1]
    chunk = swap_ref.shape[0]
    x = iota((chunk, total), 0) + i * chunk
    y = iota((chunk, total), 1)
    swap_ref[...] = (x == (y % occ) * occ + y // occ).astype(F32).astype(BF16)

    for j in range(tile // rows):
        o = i * (tile // rows) + j
        equal = iota((rows, rows), 0) == place_ref[o]
        for c in range(bc):
            hit = equal & (live_ref[i * bc + c] > 0)
            one_hot = hit.astype(F32).astype(BF16)
            got = jnp.dot(one_hot, tiles[c][0, 0, 0, j * rows : (j + 1) * rows, :], preferred_element_type=F32)
            at = slice(c * tile, (c + 1) * tile)
            u_ref[j, :, at] = got[:own].astype(BF16)
            for d in range(1, n):
                a = lax.rem(o + d, n)
                start = (n - d - 1) * half
                w_ref[a, start : start + half, at] = got[own + (d - 1) * half : own + d * half].astype(BF16)


def reduce_kernel(
    n, half, ranks, u_hbm, w_hbm, swap_hbm, *refs
):
    pieces, refs = refs[:ranks], refs[ranks:]
    (
        z_ref, ubuf, wbuf, tall, t2buf, swap, sbuf, q1s, s1s, q1r, s1r, q2s, s2s, q2r, s2r, xqs, xss, xqr, xsr,
        usem, wsem, tsem, psem, q1a, q1b, s1a, s1b, q2a, q2b, s2a, s2b, xqa, xqb, xsa, xsb,
    ) = refs
    me = lax.axis_index("col")
    row = lax.axis_index("row")
    levels = n // 2
    level, side = me // 2, lax.rem(me, 2)
    other = me + 1 - 2 * side
    bc, tile, width = tall.shape
    depth = bc * tile
    share = tile // ranks
    own = (n + 1) * half
    chunks = n + 1

    def load_t(k):
        source = lax.rem(row + 2 * (k // 2), ranks)
        source = source if k % 2 == 0 else source + 1 - 2 * lax.rem(source, 2)
        first = pl.multiple_of(source * share, share)
        return pltpu.make_async_copy(pieces[k], tall.at[:, pl.ds(first, share), :], tsem.at[k])

    load_p = pltpu.make_async_copy(swap_hbm, swap, psem)
    for k in range(ranks):
        load_t(k).start()
    load_p.start()

    def load(a):
        return (
            pltpu.make_async_copy(u_hbm.at[a], ubuf.at[a], usem.at[a]),
            pltpu.make_async_copy(w_hbm.at[a], wbuf.at[a], wsem.at[a]),
        )

    def owner(k, of_side):
        return 2 * lax.rem(level + 1 + k, levels) + of_side

    for of_side in (1 - side, side):
        for k in range(levels):
            for copy in load(owner(k, of_side)):
                copy.start()

    barrier = pltpu.get_barrier_semaphore()
    for d in range(1, n):
        pl.semaphore_signal(barrier, inc=1, device_id={"col": lax.rem(me + d, n)}, device_id_type=MESH)
    pl.semaphore_wait(barrier, n - 1)

    for k in range(ranks):
        load_t(k).wait()
    load_p.wait()
    high = 256
    per = tile // high

    @pl.loop(0, depth // high)
    def _(k):
        at = pl.ds(pl.multiple_of(k * high, high), high)
        source = tall.at[k // per, pl.ds(pl.multiple_of(lax.rem(k, per) * high, high), high), :]
        for c in range(0, width, 256):
            t2buf[at, c : c + 256] = jnp.dot(source[...], swap[:, c : c + 256], preferred_element_type=F32).astype(BF16)

    def product(a, out):
        for copy in load(a):
            copy.wait()

        @pl.loop(0, width // 256)
        def _(c):
            at = pl.ds(pl.multiple_of(c * 256, 256), 256)
            first = jnp.dot(ubuf[a], tall[:, :, at].reshape(depth, 256), preferred_element_type=F32)
            second = jnp.dot(wbuf[a], t2buf[:, at], preferred_element_type=F32)
            out[0 : 2 * half, at] = first[: 2 * half]
            out[2 * half : own, at] = first[2 * half :] + second

    def remote(source, target, sent, arrived, device):
        return pltpu.make_async_remote_copy(
            src_ref=source, dst_ref=target, send_sem=sent, recv_sem=arrived,
            device_id={"col": device}, device_id_type=MESH,
        )

    def first_copy(k):
        return (
            remote(q1s.at[k], q1r.at[k], q1a.at[k], q1b.at[k], other),
            remote(s1s.at[k], s1r.at[k], s1a.at[k], s1b.at[k], other),
        )

    def second_copy(k):
        device = owner(k, side)
        return (
            remote(q2s.at[k], q2r.at[k], q2a.at[k], q2b.at[k], device),
            remote(s2s.at[k], s2r.at[k], s2a.at[k], s2b.at[k], device),
        )

    diagonal = iota((half, 128), 0) == iota((half, 128), 1)

    def to_levels(part):
        most = jnp.max(jnp.abs(part), axis=1, keepdims=True)
        inverse = jnp.where(most > 1e-30, LEVELS / jnp.maximum(most, 1e-30), 0.0)
        scale = jnp.sum(jnp.where(diagonal, most * (1.0 / LEVELS), 0.0), axis=0, keepdims=True)
        return jnp.round(part * inverse).astype(I32).astype(I16), scale

    def from_levels(value, scale):
        return value.astype(I32).astype(F32) * jnp.sum(jnp.where(diagonal, scale, 0.0), axis=1, keepdims=True)

    @pl.loop(0, levels)
    def _(k):
        product(owner(k, 1 - side), sbuf)
        for m in range(chunks):
            q1s[k, m], s1s[k, m : m + 1, :] = to_levels(sbuf[m * half : (m + 1) * half, :])
        for copy in first_copy(k):
            copy.start()

    @pl.loop(0, levels - 1)
    def _(k):
        product(owner(k, side), sbuf)
        for copy in first_copy(k):
            copy.wait_recv()
        for m in range(chunks):
            part = sbuf[m * half : (m + 1) * half, :] + from_levels(q1r[k, m], s1r[k, m : m + 1, :])
            q2s[k, m], s2s[k, m : m + 1, :] = to_levels(part)
        for copy in second_copy(k):
            copy.start()

    product(me, z_ref)

    def take(k, value, scale):
        for m in range(chunks):
            z_ref[m * half : (m + 1) * half, :] += from_levels(value[k, m], scale[k, m : m + 1, :])

    for copy in first_copy(levels - 1):
        copy.wait_recv()
    take(levels - 1, q1r, s1r)

    @pl.loop(0, levels - 1)
    def _(k):
        for copy in second_copy(k):
            copy.wait_recv()
        take(k, q2r, s2r)

    def last_copy(d):
        device = lax.rem(me + d, n)
        return (
            remote(xqs.at[d], xqr.at[n - d], xqa.at[d], xqb.at[n - d], device),
            remote(xss.at[d], xsr.at[n - d], xsa.at[d], xsb.at[n - d], device),
        )

    for d in range(1, n):
        xqs[d], xss[d, 0:1, :] = to_levels(z_ref[(d + 1) * half : (d + 2) * half, :])
        for copy in last_copy(d):
            copy.start()
    for d in range(1, n):
        for copy in last_copy(d):
            copy.wait_recv()
    for d in range(1, n):
        z_ref[own + (d - 1) * half : own + d * half, :] = from_levels(xqr[d], xsr[d, 0:1, :])
    for d in range(1, n):
        for copy in last_copy(d):
            copy.wait_send()

    @pl.loop(0, levels)
    def _(k):
        for copy in first_copy(k):
            copy.wait_send()

    @pl.loop(0, levels - 1)
    def _(k):
        for copy in second_copy(k):
            copy.wait_send()


def final_kernel(half, own, z_ref, swap_ref, place_ref, mirror_ref, pair_ref, occ_ref, out_ref, pieces):
    rows, width = z_ref.shape

    @pl.when(pl.program_id(0) == 0)
    def _():
        rest = z_ref[...]
        for p in range(2):
            piece = rest.astype(BF16)
            pieces[p] = piece
            rest = rest - piece.astype(F32)

    chunk = out_ref.shape[1]
    at = pl.ds(pl.multiple_of(pl.program_id(0) * chunk, chunk), chunk)
    place, mirror = place_ref[...], mirror_ref[...]

    def hot(count, first):
        number = iota((rows, count), 1) + first
        return ((number == place) | (number == mirror)).astype(F32).astype(BF16)

    hot_own, hot_far, hot_self = hot(own, 0), hot(rows - own, own), hot(2 * half, rows)
    mixer = swap_ref[...]
    total = None
    for p in (1, 0):
        far = jnp.dot(pieces[p, own:, :], mixer, preferred_element_type=F32).astype(BF16)
        near = jnp.dot(pieces[p, : 2 * half, :], mixer, preferred_element_type=F32).astype(BF16)
        term = jnp.dot(hot_own, pieces[p, :own, at], preferred_element_type=F32)
        mine = jnp.dot(hot_self, near, preferred_element_type=F32)
        other = jnp.dot(hot_far, far, preferred_element_type=F32)
        term = term + (mine + other)
        total = term if total is None else total + term
    out_ref[...] = total / (pair_ref[...] - occ_ref[...])


def body(integrals, tile_count, tile_list, amplitudes, pair_energy, occ_energy, partner):
    n = lax.axis_size("col")
    me = lax.axis_index("col")
    rows = partner.shape[0]
    half = rows // n // 2
    own = (n + 1) * half
    slots, tile = integrals.shape[2], integrals.shape[3]
    bc, _, width = amplitudes.shape
    br = slots // bc
    occ = occ_energy.shape[0]
    depth = bc * tile

    place, mirror = row_places(partner, me, n)
    ranks = lax.axis_size("row")
    pieces = [amplitudes]
    for k in range(2, ranks, 2):
        pieces.append(lax.ppermute(amplitudes, "row", [((r + k) % ranks, r) for r in range(ranks)]))
    pieces = [q for p in pieces for q in (p, lax.ppermute(p, "row", [(r ^ 1, r) for r in range(ranks)]))]

    dma = pltpu.SemaphoreType.DMA
    places = pl.pallas_call(
        functools.partial(gather_kernel, n),
        out_shape=jax.ShapeDtypeStruct((n, 1, rows), I32),
        in_specs=[pl.BlockSpec(memory_space=pltpu.VMEM)],
        out_specs=pl.BlockSpec(memory_space=pltpu.VMEM),
        scratch_shapes=[pltpu.VMEM((n, 1, rows), I32), dma((n,)), dma((n,))],
        compiler_params=pltpu.CompilerParams(collective_id=1, has_side_effects=True),
        name="gather_places",
    )(place[None, :])

    number = jnp.arange(slots, dtype=I32)
    slot = jnp.sum(jnp.where(tile_list[0, 0][None, :] == number[:, None], number[None, :], 0), axis=1)
    live = (slot < tile_count[0, 0]).astype(I32)

    per = tile // rows

    def tile_spec(c):
        return pl.BlockSpec((1, 1, 1, tile, tile), lambda i, s, l: (0, 0, s[i * bc + c], 0, 0))

    u, w, swap = pl.pallas_call(
        functools.partial(sort_kernel, n, half, occ, bc),
        grid_spec=pltpu.PrefetchScalarGridSpec(
            num_scalar_prefetch=2,
            grid=(br,),
            in_specs=[tile_spec(c) for c in range(bc)] + [pl.BlockSpec((n, 1, rows), lambda i, s, l: (0, 0, 0))],
            out_specs=[
                pl.BlockSpec((per, own, depth), lambda i, s, l: (i, 0, 0)),
                pl.BlockSpec((n, rows - own, depth), lambda i, s, l: (0, 0, 0)),
                pl.BlockSpec((width // br, width), lambda i, s, l: (i, 0)),
            ],
        ),
        out_shape=[
            jax.ShapeDtypeStruct((n, own, depth), BF16),
            jax.ShapeDtypeStruct((n, rows - own, depth), BF16),
            jax.ShapeDtypeStruct((width, width), BF16),
        ],
        compiler_params=pltpu.CompilerParams(vmem_limit_bytes=48 * 1024 * 1024),
        cost_estimate=pl.CostEstimate(
            flops=2 * slots * rows * tile * tile, bytes_accessed=4 * slots * tile * tile, transcendentals=0
        ),
        name="sort_rows",
    )(slot, live, *([integrals] * bc), places)

    anywhere = pl.BlockSpec(memory_space=pl.ANY)
    scale_rows = -(-(n + 1) // 8) * 8
    levels = n // 2
    packed = [pltpu.VMEM((levels, n + 1, half, width), I16), pltpu.VMEM((levels, scale_rows, 128), F32)]
    last = [pltpu.VMEM((n, half, width), I16), pltpu.VMEM((n, 8, 128), F32)]
    z = pl.pallas_call(
        functools.partial(reduce_kernel, n, half, ranks),
        out_shape=jax.ShapeDtypeStruct((rows, width), F32),
        in_specs=[anywhere] * (3 + ranks),
        out_specs=pl.BlockSpec(memory_space=pltpu.VMEM),
        scratch_shapes=[
            pltpu.VMEM((n, own, depth), BF16),
            pltpu.VMEM((n, rows - own, depth), BF16),
            pltpu.VMEM((bc, tile, width), BF16),
            pltpu.VMEM((depth, width), BF16),
            pltpu.VMEM((width, width), BF16),
            pltpu.VMEM((own, width), F32),
            *(packed * 4),
            *(last * 2),
            dma((n,)), dma((n,)), dma((ranks,)), dma,
            *([dma((levels,))] * 8),
            *([dma((n,))] * 4),
        ],
        compiler_params=pltpu.CompilerParams(
            collective_id=0, has_side_effects=True, vmem_limit_bytes=63 * 1024 * 1024
        ),
        name="reduce_pairs",
    )(u, w, swap, *pieces)

    chunk = 256
    whole = lambda k: (0, 0)
    return pl.pallas_call(
        functools.partial(final_kernel, half, own),
        grid=(width // chunk,),
        in_specs=[
            pl.BlockSpec((rows, width), whole),
            pl.BlockSpec((width, chunk), lambda k: (0, k)),
            pl.BlockSpec((rows, 1), whole),
            pl.BlockSpec((rows, 1), whole),
            pl.BlockSpec((rows, 1), whole),
            pl.BlockSpec((1, chunk), lambda k: (0, k)),
        ],
        out_specs=pl.BlockSpec((rows, chunk), lambda k: (0, k)),
        out_shape=jax.ShapeDtypeStruct((rows, width), F32),
        scratch_shapes=[pltpu.VMEM((2, rows, width), BF16)],
        compiler_params=pltpu.CompilerParams(vmem_limit_bytes=40 * 1024 * 1024),
        name="finish_rows",
    )(
        z, swap, place[:, None], mirror[:, None], pair_energy[:, None],
        (occ_energy[:, None] + occ_energy[None, :]).reshape(1, width),
    )


def solution(mesh):
    return jax.shard_map(
        body,
        mesh=mesh,
        in_specs=(
            P("row", "col", None, None, None),
            P("row", "col"),
            P("row", "col", None),
            P("col", "row", None),
            P(("row", "col")),
            P(),
            P(("row", "col")),
        ),
        out_specs=P(("row", "col"), None),
        check_vma=False,
    )
```

```python
import functools

import jax
import jax.numpy as jnp
from jax import lax
from jax.experimental import pallas as pl
from jax.experimental.pallas import tpu as pltpu
from jax.sharding import PartitionSpec as P

MESH = pl.DeviceIdType.MESH
F32, BF16, I32, I16 = jnp.float32, jnp.bfloat16, jnp.int32, jnp.int16
LEVELS = 32767.0


def iota(shape, axis):
    return lax.broadcasted_iota(I32, shape, axis)


def row_places(partner, me, n):
    rows = partner.shape[0]
    half = rows // n // 2
    own = (n + 1) * half
    local = partner % (n * rows)
    block, within = local // rows, local % rows
    index = jnp.arange(rows, dtype=I32)
    key = jnp.where(block < me, within, index)
    before = (block[None, :] == block[:, None]) & (key[None, :] < key[:, None])
    rank = jnp.sum(before.astype(I32), axis=1)
    shift = (block - me + n) % n
    owned = jnp.where(me < block, rank < half, rank >= half)
    step = (shift - 1) * half + rank % half
    place = jnp.where(block == me, rank, jnp.where(owned, 2 * half + step, own + step))
    found = jnp.sum(jnp.where(index[None, :] == within[:, None], place[None, :], 0), axis=1)
    mirror = jnp.where(block == me, rows + found, -1)
    return place, mirror


def gather_kernel(n, mine_ref, all_ref, landed, send_sem, recv_sem):
    me = lax.axis_index("col")
    barrier = pltpu.get_barrier_semaphore()
    for d in range(1, n):
        pl.semaphore_signal(barrier, inc=1, device_id={"col": lax.rem(me + d, n)}, device_id_type=MESH)
    pl.semaphore_wait(barrier, n - 1)

    def copy(d):
        return pltpu.make_async_remote_copy(
            src_ref=mine_ref, dst_ref=landed.at[d], send_sem=send_sem.at[d], recv_sem=recv_sem.at[d],
            device_id={"col": lax.rem(me + d, n)}, device_id_type=MESH,
        )

    for d in range(1, n):
        copy(d).start()
    all_ref[me] = mine_ref[...]
    for d in range(1, n):
        copy(d).wait_recv()
        all_ref[lax.rem(me + n - d, n)] = landed[d]
    for d in range(1, n):
        copy(d).wait_send()


def sort_kernel(n, half, occ, bc, slot_ref, live_ref, *refs):
    tiles, (place_ref, u_ref, w_ref, swap_ref) = refs[:bc], refs[bc:]
    i = pl.program_id(0)
    rows = place_ref.shape[2]
    tile = tiles[0].shape[3]
    own = (n + 1) * half

    total = swap_ref.shape[1]
    chunk = swap_ref.shape[0]
    x = iota((chunk, total), 0) + i * chunk
    y = iota((chunk, total), 1)
    swap_ref[...] = (x == (y % occ) * occ + y // occ).astype(F32).astype(BF16)

    for j in range(tile // rows):
        o = i * (tile // rows) + j
        equal = iota((rows, rows), 0) == place_ref[o]
        for c in range(bc):
            hit = equal & (live_ref[i * bc + c] > 0)
            one_hot = hit.astype(F32).astype(BF16)
            got = jnp.dot(one_hot, tiles[c][0, 0, 0, j * rows : (j + 1) * rows, :], preferred_element_type=F32)
            at = slice(c * tile, (c + 1) * tile)
            u_ref[j, :, at] = got[:own].astype(BF16)
            for d in range(1, n):
                a = lax.rem(o + d, n)
                start = (n - d - 1) * half
                w_ref[a, start : start + half, at] = got[own + (d - 1) * half : own + d * half].astype(BF16)


def reduce_kernel(
    n, half, ranks, wide, u_hbm, w_hbm, swap_hbm, *refs
):
    held = ranks // 2 + 1
    given, refs = refs[:held], refs[held:]
    pieces = [given[0], given[1]]
    for piece in given[2:]:
        pieces += [piece, None]
    (
        z_ref, ubuf, wbuf, tall, t2buf, swap, sbuf, q1s, s1s, q1r, s1r, q2s, s2s, q2r, s2r, xqs, xss, xqr, xsr,
        usem, wsem, tsem, psem, q1a, q1b, s1a, s1b, q2a, q2b, s2a, s2b, xqa, xqb, xsa, xsb, psend, precv,
    ) = refs
    me = lax.axis_index("col")
    row = lax.axis_index("row")
    levels = n // 2
    level, side = me // 2, lax.rem(me, 2)
    other = me + 1 - 2 * side
    bc, tile, width = tall.shape
    depth = bc * tile
    share = tile // ranks
    own = (n + 1) * half
    chunks = n + 1

    def load_t(k):
        source = lax.rem(row + 2 * (k // 2), ranks)
        source = source if k % 2 == 0 else source + 1 - 2 * lax.rem(source, 2)
        first = pl.multiple_of(source * share, share)
        return pltpu.make_async_copy(pieces[k], tall.at[:, pl.ds(first, share), :], tsem.at[k])

    def swap_t(k):
        first = pl.multiple_of(lax.rem(row + 2 * (k // 2), ranks) * share, share)
        return pltpu.make_async_remote_copy(
            src_ref=pieces[k], dst_ref=tall.at[:, pl.ds(first, share), :], send_sem=psend.at[k], recv_sem=precv.at[k],
            device_id={"row": row + 1 - 2 * lax.rem(row, 2)}, device_id_type=MESH,
        )

    local = [k for k in range(ranks) if pieces[k] is not None]
    crossed = [k - 1 for k in range(ranks) if pieces[k] is None]
    load_p = pltpu.make_async_copy(swap_hbm, swap, psem)
    for k in local:
        load_t(k).start()
    load_p.start()

    def load(a):
        return (
            pltpu.make_async_copy(u_hbm.at[a], ubuf.at[a], usem.at[a]),
            pltpu.make_async_copy(w_hbm.at[a], wbuf.at[a], wsem.at[a]),
        )

    def owner(k, of_side):
        return 2 * lax.rem(level + 1 + k, levels) + of_side

    for of_side in (1 - side, side):
        for k in range(levels):
            for copy in load(owner(k, of_side)):
                copy.start()

    barrier = pltpu.get_barrier_semaphore()
    for d in range(1, n):
        pl.semaphore_signal(barrier, inc=1, device_id={"col": lax.rem(me + d, n)}, device_id_type=MESH)
    pl.semaphore_signal(barrier, inc=1, device_id={"row": row + 1 - 2 * lax.rem(row, 2)}, device_id_type=MESH)
    pl.semaphore_wait(barrier, n)

    for k in crossed:
        swap_t(k).start()
    for k in local:
        load_t(k).wait()
    load_p.wait()
    for k in crossed:
        swap_t(k).wait_recv()
    high = 256
    per = tile // high
    parts = width // wide

    def columns(c):
        return pl.ds(pl.multiple_of(c * wide, wide), wide)

    def product(a, c, out, out_at):
        at = columns(c)
        first = jnp.dot(ubuf[a], tall[:, :, at].reshape(depth, wide), preferred_element_type=F32)
        second = jnp.dot(wbuf[a], t2buf[:, at], preferred_element_type=F32)
        out[0 : 2 * half, out_at] = first[: 2 * half]
        out[2 * half : own, out_at] = first[2 * half :] + second

    def remote(source, target, sent, arrived, device):
        return pltpu.make_async_remote_copy(
            src_ref=source, dst_ref=target, send_sem=sent, recv_sem=arrived,
            device_id={"col": device}, device_id_type=MESH,
        )

    def first_copy(c, k):
        u = c * levels + k
        return (
            remote(q1s.at[u], q1r.at[u], q1a.at[u], q1b.at[u], other),
            remote(s1s.at[u], s1r.at[u], s1a.at[u], s1b.at[u], other),
        )

    def second_copy(c, k):
        device = owner(k, side)
        u = c * levels + k
        return (
            remote(q2s.at[u], q2r.at[u], q2a.at[u], q2b.at[u], device),
            remote(s2s.at[u], s2r.at[u], s2a.at[u], s2b.at[u], device),
        )

    def last_copy(c, d):
        device = lax.rem(me + d, n)
        u, v = c * n + d, c * n + n - d
        return (
            remote(xqs.at[u], xqr.at[v], xqa.at[u], xqb.at[v], device),
            remote(xss.at[u], xsr.at[v], xsa.at[u], xsb.at[v], device),
        )

    group = 128 // half
    lane, line = iota((half, 128), 1), iota((half, 128), 0)

    def to_levels(part, m):
        most = jnp.max(jnp.abs(part), axis=1, keepdims=True)
        inverse = jnp.where(most > 1e-30, LEVELS / jnp.maximum(most, 1e-30), 0.0)
        here = lane == line + (m % group) * half
        scale = jnp.sum(jnp.where(here, most * (1.0 / LEVELS), 0.0), axis=0, keepdims=True)
        return jnp.round(part * inverse).astype(I32).astype(I16), scale

    def from_levels(value, scale, m):
        here = lane == line + (m % group) * half
        return value.astype(I32).astype(F32) * jnp.sum(jnp.where(here, scale, 0.0), axis=1, keepdims=True)

    def pack(u, value, q, s):
        for g in range(0, chunks, group):
            line_of = None
            for m in range(g, min(g + group, chunks)):
                q[u, m], scale = to_levels(value(m), m)
                line_of = scale if line_of is None else line_of + scale
            s[u, g // group : g // group + 1, :] = line_of

    def unpack(u, m, q, s):
        return from_levels(q[u, m], s[u, m // group : m // group + 1, :], m)

    def rows_of(m):
        return slice(m * half, (m + 1) * half)

    @pl.loop(0, parts + 2)
    def _(turn):
        @pl.when(turn < parts)
        def _():
            at = columns(turn)

            @pl.loop(0, depth // high)
            def _(k):
                source = tall.at[k // per, pl.ds(pl.multiple_of(lax.rem(k, per) * high, high), high), :]
                t2buf[pl.ds(pl.multiple_of(k * high, high), high), at] = jnp.dot(
                    source[...], swap[:, at], preferred_element_type=F32
                ).astype(BF16)

            @pl.loop(0, levels)
            def _(k):
                @pl.when(turn == 0)
                def _():
                    for copy in load(owner(k, 1 - side)):
                        copy.wait()

                product(owner(k, 1 - side), turn, sbuf, slice(None))
                pack(turn * levels + k, lambda m: sbuf[rows_of(m), :], q1s, s1s)
                for copy in first_copy(turn, k):
                    copy.start()

        @pl.when((turn >= 1) & (turn <= parts))
        def _():
            c = turn - 1

            @pl.loop(0, levels - 1)
            def _(k):
                @pl.when(c == 0)
                def _():
                    for copy in load(owner(k, side)):
                        copy.wait()

                product(owner(k, side), c, sbuf, slice(None))
                for copy in first_copy(c, k):
                    copy.wait_recv()
                u = c * levels + k
                pack(u, lambda m: sbuf[rows_of(m), :] + unpack(u, m, q1r, s1r), q2s, s2s)
                for copy in second_copy(c, k):
                    copy.start()

        @pl.when(turn >= 2)
        def _():
            c = turn - 2

            @pl.when(c == 0)
            def _():
                for copy in load(me):
                    copy.wait()

            at = columns(c)
            product(me, c, z_ref, at)

            def take(k, q, s):
                for m in range(chunks):
                    z_ref[rows_of(m), at] += unpack(c * levels + k, m, q, s)

            for copy in first_copy(c, levels - 1):
                copy.wait_recv()
            take(levels - 1, q1r, s1r)

            @pl.loop(0, levels - 1)
            def _(k):
                for copy in second_copy(c, k):
                    copy.wait_recv()
                take(k, q2r, s2r)

            for d in range(1, n):
                xqs[c * n + d], xss[c * n + d] = to_levels(z_ref[rows_of(d + 1), at], 0)
                for copy in last_copy(c, d):
                    copy.start()

    @pl.loop(0, parts)
    def _(c):
        for d in range(1, n):
            for copy in last_copy(c, d):
                copy.wait_recv()
            v = n - d
            z_ref[own + (v - 1) * half : own + v * half, columns(c)] = from_levels(xqr[c * n + v], xsr[c * n + v], 0)

    for k in crossed:
        swap_t(k).wait_send()

    @pl.loop(0, parts)
    def _(c):
        for d in range(1, n):
            for copy in last_copy(c, d):
                copy.wait_send()

        @pl.loop(0, levels)
        def _(k):
            for copy in first_copy(c, k):
                copy.wait_send()

        @pl.loop(0, levels - 1)
        def _(k):
            for copy in second_copy(c, k):
                copy.wait_send()


def final_kernel(half, own, z_ref, swap_ref, place_ref, mirror_ref, pair_ref, occ_ref, out_ref, pieces):
    rows, width = z_ref.shape

    @pl.when(pl.program_id(0) == 0)
    def _():
        rest = z_ref[...]
        for p in range(2):
            piece = rest.astype(BF16)
            pieces[p] = piece
            rest = rest - piece.astype(F32)

    chunk = out_ref.shape[1]
    at = pl.ds(pl.multiple_of(pl.program_id(0) * chunk, chunk), chunk)
    place, mirror = place_ref[...], mirror_ref[...]

    def hot(count, first):
        number = iota((rows, count), 1) + first
        return ((number == place) | (number == mirror)).astype(F32).astype(BF16)

    hot_own, hot_far, hot_self = hot(own, 0), hot(rows - own, own), hot(2 * half, rows)
    mixer = swap_ref[...]
    total = None
    for p in (1, 0):
        far = jnp.dot(pieces[p, own:, :], mixer, preferred_element_type=F32).astype(BF16)
        near = jnp.dot(pieces[p, : 2 * half, :], mixer, preferred_element_type=F32).astype(BF16)
        term = jnp.dot(hot_own, pieces[p, :own, at], preferred_element_type=F32)
        mine = jnp.dot(hot_self, near, preferred_element_type=F32)
        other = jnp.dot(hot_far, far, preferred_element_type=F32)
        term = term + (mine + other)
        total = term if total is None else total + term
    out_ref[...] = total / (pair_ref[...] - occ_ref[...])


def body(integrals, tile_count, tile_list, amplitudes, pair_energy, occ_energy, partner):
    n = lax.axis_size("col")
    me = lax.axis_index("col")
    rows = partner.shape[0]
    half = rows // n // 2
    own = (n + 1) * half
    slots, tile = integrals.shape[2], integrals.shape[3]
    bc, _, width = amplitudes.shape
    br = slots // bc
    occ = occ_energy.shape[0]
    depth = bc * tile

    place, mirror = row_places(partner, me, n)
    ranks = lax.axis_size("row")
    pieces = [amplitudes, lax.ppermute(amplitudes, "row", [(r ^ 1, r) for r in range(ranks)])]
    for k in range(2, ranks, 2):
        pieces.append(lax.ppermute(amplitudes, "row", [((r + k) % ranks, r) for r in range(ranks)]))

    dma = pltpu.SemaphoreType.DMA
    places = pl.pallas_call(
        functools.partial(gather_kernel, n),
        out_shape=jax.ShapeDtypeStruct((n, 1, rows), I32),
        in_specs=[pl.BlockSpec(memory_space=pltpu.VMEM)],
        out_specs=pl.BlockSpec(memory_space=pltpu.VMEM),
        scratch_shapes=[pltpu.VMEM((n, 1, rows), I32), dma((n,)), dma((n,))],
        compiler_params=pltpu.CompilerParams(collective_id=1, has_side_effects=True),
        name="gather_places",
    )(place[None, :])

    number = jnp.arange(slots, dtype=I32)
    slot = jnp.sum(jnp.where(tile_list[0, 0][None, :] == number[:, None], number[None, :], 0), axis=1)
    live = (slot < tile_count[0, 0]).astype(I32)

    per = tile // rows

    def tile_spec(c):
        return pl.BlockSpec((1, 1, 1, tile, tile), lambda i, s, l: (0, 0, s[i * bc + c], 0, 0))

    u, w, swap = pl.pallas_call(
        functools.partial(sort_kernel, n, half, occ, bc),
        grid_spec=pltpu.PrefetchScalarGridSpec(
            num_scalar_prefetch=2,
            grid=(br,),
            in_specs=[tile_spec(c) for c in range(bc)] + [pl.BlockSpec((n, 1, rows), lambda i, s, l: (0, 0, 0))],
            out_specs=[
                pl.BlockSpec((per, own, depth), lambda i, s, l: (i, 0, 0)),
                pl.BlockSpec((n, rows - own, depth), lambda i, s, l: (0, 0, 0)),
                pl.BlockSpec((width // br, width), lambda i, s, l: (i, 0)),
            ],
        ),
        out_shape=[
            jax.ShapeDtypeStruct((n, own, depth), BF16),
            jax.ShapeDtypeStruct((n, rows - own, depth), BF16),
            jax.ShapeDtypeStruct((width, width), BF16),
        ],
        compiler_params=pltpu.CompilerParams(vmem_limit_bytes=63 * 1024 * 1024),
        cost_estimate=pl.CostEstimate(
            flops=2 * slots * rows * tile * tile, bytes_accessed=4 * slots * tile * tile, transcendentals=0
        ),
        name="sort_rows",
    )(slot, live, *([integrals] * bc), places)

    anywhere = pl.BlockSpec(memory_space=pl.ANY)
    wide = 256
    parts = width // wide
    scale_rows = -(-(n + 1) // (128 // half))
    units = parts * (n // 2)
    packed = [pltpu.VMEM((units, n + 1, half, wide), I16), pltpu.VMEM((units, scale_rows, 128), F32)]
    last = [pltpu.VMEM((parts * n, half, wide), I16), pltpu.VMEM((parts * n, 1, 128), F32)]
    z = pl.pallas_call(
        functools.partial(reduce_kernel, n, half, ranks, wide),
        out_shape=jax.ShapeDtypeStruct((rows, width), F32),
        in_specs=[anywhere] * (3 + len(pieces)),
        out_specs=pl.BlockSpec(memory_space=pltpu.VMEM),
        scratch_shapes=[
            pltpu.VMEM((n, own, depth), BF16),
            pltpu.VMEM((n, rows - own, depth), BF16),
            pltpu.VMEM((bc, tile, width), BF16),
            pltpu.VMEM((depth, width), BF16),
            pltpu.VMEM((width, width), BF16),
            pltpu.VMEM((own, wide), F32),
            *(packed * 4),
            *(last * 2),
            dma((n,)), dma((n,)), dma((ranks,)), dma,
            *([dma((units,))] * 8),
            *([dma((parts * n,))] * 4),
            dma((ranks,)), dma((ranks,)),
        ],
        compiler_params=pltpu.CompilerParams(
            collective_id=0, has_side_effects=True, vmem_limit_bytes=63 * 1024 * 1024
        ),
        name="reduce_pairs",
    )(u, w, swap, *pieces)

    chunk = 256
    whole = lambda k: (0, 0)
    return pl.pallas_call(
        functools.partial(final_kernel, half, own),
        grid=(width // chunk,),
        in_specs=[
            pl.BlockSpec((rows, width), whole),
            pl.BlockSpec((width, chunk), lambda k: (0, k)),
            pl.BlockSpec((rows, 1), whole),
            pl.BlockSpec((rows, 1), whole),
            pl.BlockSpec((rows, 1), whole),
            pl.BlockSpec((1, chunk), lambda k: (0, k)),
        ],
        out_specs=pl.BlockSpec((rows, chunk), lambda k: (0, k)),
        out_shape=jax.ShapeDtypeStruct((rows, width), F32),
        scratch_shapes=[pltpu.VMEM((2, rows, width), BF16)],
        compiler_params=pltpu.CompilerParams(vmem_limit_bytes=63 * 1024 * 1024),
        name="finish_rows",
    )(
        z, swap, place[:, None], mirror[:, None], pair_energy[:, None],
        (occ_energy[:, None] + occ_energy[None, :]).reshape(1, width),
    )


def solution(mesh):
    return jax.shard_map(
        body,
        mesh=mesh,
        in_specs=(
            P("row", "col", None, None, None),
            P("row", "col"),
            P("row", "col", None),
            P("col", "row", None),
            P(("row", "col")),
            P(),
            P(("row", "col")),
        ),
        out_specs=P(("row", "col"), None),
        check_vma=False,
    )
```

```python
import functools

import jax
import jax.numpy as jnp
from jax import lax
from jax.experimental import pallas as pl
from jax.experimental.pallas import tpu as pltpu
from jax.sharding import PartitionSpec as P

MESH = pl.DeviceIdType.MESH
F32, BF16, I32, I16 = jnp.float32, jnp.bfloat16, jnp.int32, jnp.int16
LEVELS = 32767.0


def iota(shape, axis):
    return lax.broadcasted_iota(I32, shape, axis)


def row_places(partner, me, n):
    rows = partner.shape[0]
    half = rows // n // 2
    own = (n + 1) * half
    local = partner % (n * rows)
    block, within = local // rows, local % rows
    index = jnp.arange(rows, dtype=I32)
    key = jnp.where(block < me, within, index)
    before = (block[None, :] == block[:, None]) & (key[None, :] < key[:, None])
    rank = jnp.sum(before.astype(I32), axis=1)
    shift = (block - me + n) % n
    owned = jnp.where(me < block, rank < half, rank >= half)
    step = (shift - 1) * half + rank % half
    place = jnp.where(block == me, rank, jnp.where(owned, 2 * half + step, own + step))
    found = jnp.sum(jnp.where(index[None, :] == within[:, None], place[None, :], 0), axis=1)
    mirror = jnp.where(block == me, rows + found, -1)
    return place, mirror


def gather_kernel(n, mine_ref, all_ref, landed, send_sem, recv_sem):
    me = lax.axis_index("col")
    barrier = pltpu.get_barrier_semaphore()
    for d in range(1, n):
        pl.semaphore_signal(barrier, inc=1, device_id={"col": lax.rem(me + d, n)}, device_id_type=MESH)
    pl.semaphore_wait(barrier, n - 1)

    def copy(d):
        return pltpu.make_async_remote_copy(
            src_ref=mine_ref, dst_ref=landed.at[d], send_sem=send_sem.at[d], recv_sem=recv_sem.at[d],
            device_id={"col": lax.rem(me + d, n)}, device_id_type=MESH,
        )

    for d in range(1, n):
        copy(d).start()
    all_ref[me] = mine_ref[...]
    for d in range(1, n):
        copy(d).wait_recv()
        all_ref[lax.rem(me + n - d, n)] = landed[d]
    for d in range(1, n):
        copy(d).wait_send()


def sort_kernel(n, half, occ, bc, slot_ref, count_ref, *refs):
    tiles, (place_ref, u_ref, w_ref, swap_ref) = refs[:bc], refs[bc:]
    i = pl.program_id(0)
    rows = place_ref.shape[2]
    tile = tiles[0].shape[3]
    own = (n + 1) * half

    total = swap_ref.shape[1]
    chunk = swap_ref.shape[0]
    x = iota((chunk, total), 0) + i * chunk
    y = iota((chunk, total), 1)
    swap_ref[...] = (x == (y % occ) * occ + y // occ).astype(F32).astype(BF16)

    for j in range(tile // rows):
        o = i * (tile // rows) + j
        equal = iota((rows, rows), 0) == place_ref[o]
        for c in range(bc):
            hit = equal & (slot_ref[i * bc + c] < count_ref[0])
            one_hot = hit.astype(F32).astype(BF16)
            got = jnp.dot(one_hot, tiles[c][0, 0, 0, j * rows : (j + 1) * rows, :], preferred_element_type=F32)
            at = slice(c * tile, (c + 1) * tile)
            u_ref[j, :, at] = got[:own].astype(BF16)
            for d in range(1, n):
                a = lax.rem(o + d, n)
                start = (n - d - 1) * half
                w_ref[a, start : start + half, at] = got[own + (d - 1) * half : own + d * half].astype(BF16)


def reduce_kernel(
    n, half, ranks, wide, u_hbm, w_hbm, swap_hbm, *refs
):
    held = ranks // 2 + 1
    given, refs = refs[:held], refs[held:]
    pieces = [given[0], given[1]]
    for piece in given[2:]:
        pieces += [piece, None]
    (
        z_ref, ubuf, wbuf, tall, t2buf, swap, sbuf, q1s, s1s, q1r, s1r, q2s, s2s, q2r, s2r, xqs, xss, xqr, xsr,
        usem, wsem, tsem, psem, q1a, q1b, s1a, s1b, q2a, q2b, s2a, s2b, xqa, xqb, xsa, xsb, psend, precv,
    ) = refs
    me = lax.axis_index("col")
    row = lax.axis_index("row")
    levels = n // 2
    level, side = me // 2, lax.rem(me, 2)
    other = me + 1 - 2 * side
    bc, tile, width = tall.shape
    depth = bc * tile
    share = tile // ranks
    own = (n + 1) * half
    chunks = n + 1

    def load_t(k):
        source = lax.rem(row + 2 * (k // 2), ranks)
        source = source if k % 2 == 0 else source + 1 - 2 * lax.rem(source, 2)
        first = pl.multiple_of(source * share, share)
        return pltpu.make_async_copy(pieces[k], tall.at[:, pl.ds(first, share), :], tsem.at[k])

    def swap_t(k):
        first = pl.multiple_of(lax.rem(row + 2 * (k // 2), ranks) * share, share)
        return pltpu.make_async_remote_copy(
            src_ref=pieces[k], dst_ref=tall.at[:, pl.ds(first, share), :], send_sem=psend.at[k], recv_sem=precv.at[k],
            device_id={"row": row + 1 - 2 * lax.rem(row, 2)}, device_id_type=MESH,
        )

    local = [k for k in range(ranks) if pieces[k] is not None]
    crossed = [k - 1 for k in range(ranks) if pieces[k] is None]
    load_p = pltpu.make_async_copy(swap_hbm, swap, psem)
    for k in local:
        load_t(k).start()
    load_p.start()

    def load(a):
        return (
            pltpu.make_async_copy(u_hbm.at[a], ubuf.at[a], usem.at[a]),
            pltpu.make_async_copy(w_hbm.at[a], wbuf.at[a], wsem.at[a]),
        )

    def owner(k, of_side):
        return 2 * lax.rem(level + 1 + k, levels) + of_side

    for copy in load(owner(0, 1 - side)):
        copy.start()

    barrier = pltpu.get_barrier_semaphore()
    for d in range(1, n):
        pl.semaphore_signal(barrier, inc=1, device_id={"col": lax.rem(me + d, n)}, device_id_type=MESH)
    pl.semaphore_signal(barrier, inc=1, device_id={"row": row + 1 - 2 * lax.rem(row, 2)}, device_id_type=MESH)
    pl.semaphore_wait(barrier, n)

    for k in crossed:
        swap_t(k).start()
    for k in local:
        load_t(k).wait()
    load_p.wait()
    for k in range(1, levels):
        for copy in load(owner(k, 1 - side)):
            copy.start()
    for k in range(levels):
        for copy in load(owner(k, side)):
            copy.start()
    for k in crossed:
        swap_t(k).wait_recv()
    high = 256
    per = tile // high
    parts = width // wide

    def columns(c):
        return pl.ds(pl.multiple_of(c * wide, wide), wide)

    def product(a, c, out, out_at):
        at = columns(c)
        first = jnp.dot(ubuf[a], tall[:, :, at].reshape(depth, wide), preferred_element_type=F32)
        second = jnp.dot(wbuf[a], t2buf[:, at], preferred_element_type=F32)
        out[0 : 2 * half, out_at] = first[: 2 * half]
        out[2 * half : own, out_at] = first[2 * half :] + second

    def remote(source, target, sent, arrived, device):
        return pltpu.make_async_remote_copy(
            src_ref=source, dst_ref=target, send_sem=sent, recv_sem=arrived,
            device_id={"col": device}, device_id_type=MESH,
        )

    def first_copy(c, k):
        u = c * levels + k
        return (
            remote(q1s.at[u], q1r.at[u], q1a.at[u], q1b.at[u], other),
            remote(s1s.at[u], s1r.at[u], s1a.at[u], s1b.at[u], other),
        )

    def second_copy(c, k):
        device = owner(k, side)
        u = c * levels + k
        return (
            remote(q2s.at[u], q2r.at[u], q2a.at[u], q2b.at[u], device),
            remote(s2s.at[u], s2r.at[u], s2a.at[u], s2b.at[u], device),
        )

    def last_copy(c, d):
        device = lax.rem(me + d, n)
        u, v = c * n + d, c * n + n - d
        return (
            remote(xqs.at[u], xqr.at[v], xqa.at[u], xqb.at[v], device),
            remote(xss.at[u], xsr.at[v], xsa.at[u], xsb.at[v], device),
        )

    group = 128 // half
    lane, line = iota((half, 128), 1), iota((half, 128), 0)

    def to_levels(part, m):
        most = jnp.max(jnp.abs(part), axis=1, keepdims=True)
        inverse = jnp.where(most > 1e-30, LEVELS / jnp.maximum(most, 1e-30), 0.0)
        here = lane == line + (m % group) * half
        scale = jnp.sum(jnp.where(here, most * (1.0 / LEVELS), 0.0), axis=0, keepdims=True)
        return jnp.round(part * inverse).astype(I32).astype(I16), scale

    def from_levels(value, scale, m):
        here = lane == line + (m % group) * half
        return value.astype(I32).astype(F32) * jnp.sum(jnp.where(here, scale, 0.0), axis=1, keepdims=True)

    def pack(u, value, q, s):
        for g in range(0, chunks, group):
            line_of = None
            for m in range(g, min(g + group, chunks)):
                q[u, m], scale = to_levels(value(m), m)
                line_of = scale if line_of is None else line_of + scale
            s[u, g // group : g // group + 1, :] = line_of

    def unpack(u, m, q, s):
        return from_levels(q[u, m], s[u, m // group : m // group + 1, :], m)

    def rows_of(m):
        return slice(m * half, (m + 1) * half)

    @pl.loop(0, parts + 2)
    def _(turn):
        @pl.when(turn < parts)
        def _():
            at = columns(turn)

            @pl.loop(0, depth // high)
            def _(k):
                source = tall.at[k // per, pl.ds(pl.multiple_of(lax.rem(k, per) * high, high), high), :]
                t2buf[pl.ds(pl.multiple_of(k * high, high), high), at] = jnp.dot(
                    source[...], swap[:, at], preferred_element_type=F32
                ).astype(BF16)

            @pl.loop(0, levels)
            def _(k):
                @pl.when(turn == 0)
                def _():
                    for copy in load(owner(k, 1 - side)):
                        copy.wait()

                product(owner(k, 1 - side), turn, sbuf, slice(None))
                pack(turn * levels + k, lambda m: sbuf[rows_of(m), :], q1s, s1s)
                for copy in first_copy(turn, k):
                    copy.start()

        @pl.when((turn >= 1) & (turn <= parts))
        def _():
            c = turn - 1

            @pl.loop(0, levels - 1)
            def _(k):
                @pl.when(c == 0)
                def _():
                    for copy in load(owner(k, side)):
                        copy.wait()

                product(owner(k, side), c, sbuf, slice(None))
                for copy in first_copy(c, k):
                    copy.wait_recv()
                u = c * levels + k
                pack(u, lambda m: sbuf[rows_of(m), :] + unpack(u, m, q1r, s1r), q2s, s2s)
                for copy in second_copy(c, k):
                    copy.start()

        @pl.when(turn >= 2)
        def _():
            c = turn - 2

            @pl.when(c == 0)
            def _():
                for copy in load(me):
                    copy.wait()

            at = columns(c)
            product(me, c, z_ref, at)

            def take(k, q, s):
                for m in range(chunks):
                    z_ref[rows_of(m), at] += unpack(c * levels + k, m, q, s)

            for copy in first_copy(c, levels - 1):
                copy.wait_recv()
            take(levels - 1, q1r, s1r)

            @pl.loop(0, levels - 1)
            def _(k):
                for copy in second_copy(c, k):
                    copy.wait_recv()
                take(k, q2r, s2r)

            for d in range(1, n):
                xqs[c * n + d], xss[c * n + d] = to_levels(z_ref[rows_of(d + 1), at], 0)
                for copy in last_copy(c, d):
                    copy.start()

    @pl.loop(0, parts)
    def _(c):
        for d in range(1, n):
            for copy in last_copy(c, d):
                copy.wait_recv()
            v = n - d
            z_ref[own + (v - 1) * half : own + v * half, columns(c)] = from_levels(xqr[c * n + v], xsr[c * n + v], 0)

    for k in crossed:
        swap_t(k).wait_send()

    @pl.loop(0, parts)
    def _(c):
        for d in range(1, n):
            for copy in last_copy(c, d):
                copy.wait_send()

        @pl.loop(0, levels)
        def _(k):
            for copy in first_copy(c, k):
                copy.wait_send()

        @pl.loop(0, levels - 1)
        def _(k):
            for copy in second_copy(c, k):
                copy.wait_send()


def final_kernel(
    half, own, z_ref, swap_ref, place_ref, mirror_ref, pair_ref, occ_ref, out_ref, pieces, hot_own, hot_far, hot_self, pair_of
):
    rows, width = z_ref.shape

    @pl.when(pl.program_id(0) == 0)
    def _():
        rest = z_ref[...]
        for p in range(2):
            piece = rest.astype(BF16)
            pieces[p] = piece
            rest = rest - piece.astype(F32)

        same = iota((rows, rows), 0) == iota((rows, rows), 1)

        def column(row):
            return jnp.sum(jnp.where(same, row, 0.0), axis=1, keepdims=True)

        place = column(place_ref[...].astype(F32)).astype(I32)
        mirror = column(mirror_ref[...].astype(F32)).astype(I32)
        pair_of[...] = jnp.broadcast_to(column(pair_ref[...]), pair_of.shape)

        def hot(out, first):
            number = iota(out.shape, 1) + first
            out[...] = ((number == place) | (number == mirror)).astype(F32).astype(BF16)

        hot(hot_own, 0)
        hot(hot_far, own)
        hot(hot_self, rows)

    chunk = out_ref.shape[1]
    at = pl.ds(pl.multiple_of(pl.program_id(0) * chunk, chunk), chunk)
    mixer = swap_ref[...]
    total = None
    for p in (1, 0):
        far = jnp.dot(pieces[p, own:, :], mixer, preferred_element_type=F32).astype(BF16)
        near = jnp.dot(pieces[p, : 2 * half, :], mixer, preferred_element_type=F32).astype(BF16)
        term = jnp.dot(hot_own[...], pieces[p, :own, at], preferred_element_type=F32)
        mine = jnp.dot(hot_self[...], near, preferred_element_type=F32)
        other = jnp.dot(hot_far[...], far, preferred_element_type=F32)
        term = term + (mine + other)
        total = term if total is None else total + term
    out_ref[...] = total / (pair_of[:, :1] - occ_ref[...])


def body(integrals, tile_count, tile_list, amplitudes, pair_energy, occ_energy, partner):
    n = lax.axis_size("col")
    me = lax.axis_index("col")
    rows = partner.shape[0]
    half = rows // n // 2
    own = (n + 1) * half
    slots, tile = integrals.shape[2], integrals.shape[3]
    bc, _, width = amplitudes.shape
    br = slots // bc
    occ = occ_energy.shape[0]
    depth = bc * tile

    place, mirror = row_places(partner, me, n)
    ranks = lax.axis_size("row")
    pieces = [amplitudes, lax.ppermute(amplitudes, "row", [(r ^ 1, r) for r in range(ranks)])]
    for k in range(2, ranks, 2):
        pieces.append(lax.ppermute(amplitudes, "row", [((r + k) % ranks, r) for r in range(ranks)]))

    dma = pltpu.SemaphoreType.DMA
    places = pl.pallas_call(
        functools.partial(gather_kernel, n),
        out_shape=jax.ShapeDtypeStruct((n, 1, rows), I32),
        in_specs=[pl.BlockSpec(memory_space=pltpu.VMEM)],
        out_specs=pl.BlockSpec(memory_space=pltpu.VMEM),
        scratch_shapes=[pltpu.VMEM((n, 1, rows), I32), dma((n,)), dma((n,))],
        compiler_params=pltpu.CompilerParams(collective_id=1, has_side_effects=True),
        name="gather_places",
    )(place[None, :])

    number = jnp.arange(slots, dtype=I32)
    slot = jnp.sum(jnp.where(tile_list[0, 0][None, :] == number[:, None], number[None, :], 0), axis=1)

    per = tile // rows

    def tile_spec(c):
        return pl.BlockSpec((1, 1, 1, tile, tile), lambda i, s, l: (0, 0, s[i * bc + c], 0, 0))

    u, w, swap = pl.pallas_call(
        functools.partial(sort_kernel, n, half, occ, bc),
        grid_spec=pltpu.PrefetchScalarGridSpec(
            num_scalar_prefetch=2,
            grid=(br,),
            in_specs=[tile_spec(c) for c in range(bc)] + [pl.BlockSpec((n, 1, rows), lambda i, s, l: (0, 0, 0))],
            out_specs=[
                pl.BlockSpec((per, own, depth), lambda i, s, l: (i, 0, 0)),
                pl.BlockSpec((n, rows - own, depth), lambda i, s, l: (0, 0, 0)),
                pl.BlockSpec((width // br, width), lambda i, s, l: (i, 0)),
            ],
        ),
        out_shape=[
            jax.ShapeDtypeStruct((n, own, depth), BF16),
            jax.ShapeDtypeStruct((n, rows - own, depth), BF16),
            jax.ShapeDtypeStruct((width, width), BF16),
        ],
        compiler_params=pltpu.CompilerParams(vmem_limit_bytes=63 * 1024 * 1024),
        cost_estimate=pl.CostEstimate(
            flops=2 * slots * rows * tile * tile, bytes_accessed=4 * slots * tile * tile, transcendentals=0
        ),
        name="sort_rows",
    )(slot, tile_count.reshape(1), *([integrals] * bc), places)

    anywhere = pl.BlockSpec(memory_space=pl.ANY)
    wide = 256
    parts = width // wide
    scale_rows = -(-(n + 1) // (128 // half))
    units = parts * (n // 2)
    packed = [pltpu.VMEM((units, n + 1, half, wide), I16), pltpu.VMEM((units, scale_rows, 128), F32)]
    last = [pltpu.VMEM((parts * n, half, wide), I16), pltpu.VMEM((parts * n, 1, 128), F32)]
    z = pl.pallas_call(
        functools.partial(reduce_kernel, n, half, ranks, wide),
        out_shape=jax.ShapeDtypeStruct((rows, width), F32),
        in_specs=[anywhere] * (3 + len(pieces)),
        out_specs=pl.BlockSpec(memory_space=pltpu.VMEM),
        scratch_shapes=[
            pltpu.VMEM((n, own, depth), BF16),
            pltpu.VMEM((n, rows - own, depth), BF16),
            pltpu.VMEM((bc, tile, width), BF16),
            pltpu.VMEM((depth, width), BF16),
            pltpu.VMEM((width, width), BF16),
            pltpu.VMEM((own, wide), F32),
            *(packed * 4),
            *(last * 2),
            dma((n,)), dma((n,)), dma((ranks,)), dma,
            *([dma((units,))] * 8),
            *([dma((parts * n,))] * 4),
            dma((ranks,)), dma((ranks,)),
        ],
        compiler_params=pltpu.CompilerParams(
            collective_id=0, has_side_effects=True, vmem_limit_bytes=63 * 1024 * 1024
        ),
        name="reduce_pairs",
    )(u, w, swap, *pieces)

    chunk = 256
    whole = lambda k: (0, 0)
    return pl.pallas_call(
        functools.partial(final_kernel, half, own),
        grid=(width // chunk,),
        in_specs=[
            pl.BlockSpec((rows, width), whole),
            pl.BlockSpec((width, chunk), lambda k: (0, k)),
            pl.BlockSpec((1, rows), whole),
            pl.BlockSpec((1, rows), whole),
            pl.BlockSpec((1, rows), whole),
            pl.BlockSpec((1, chunk), lambda k: (0, k)),
        ],
        out_specs=pl.BlockSpec((rows, chunk), lambda k: (0, k)),
        out_shape=jax.ShapeDtypeStruct((rows, width), F32),
        scratch_shapes=[
            pltpu.VMEM((2, rows, width), BF16),
            pltpu.VMEM((rows, own), BF16),
            pltpu.VMEM((rows, rows - own), BF16),
            pltpu.VMEM((rows, 2 * half), BF16),
            pltpu.VMEM((rows, 128), F32),
        ],
        compiler_params=pltpu.CompilerParams(vmem_limit_bytes=63 * 1024 * 1024),
        name="finish_rows",
    )(
        z, swap, place[None, :], mirror[None, :], pair_energy[None, :],
        (occ_energy[:, None] + occ_energy[None, :]).reshape(1, width),
    )


def solution(mesh):
    return jax.shard_map(
        body,
        mesh=mesh,
        in_specs=(
            P("row", "col", None, None, None),
            P("row", "col"),
            P("row", "col", None),
            P("col", "row", None),
            P(("row", "col")),
            P(),
            P(("row", "col")),
        ),
        out_specs=P(("row", "col"), None),
        check_vma=False,
    )
```

```python
import functools

import jax
import jax.numpy as jnp
from jax import lax
from jax.experimental import pallas as pl
from jax.experimental.pallas import tpu as pltpu
from jax.sharding import PartitionSpec as P

MESH = pl.DeviceIdType.MESH
F32, BF16, I32, I16 = jnp.float32, jnp.bfloat16, jnp.int32, jnp.int16
LEVELS = 32767.0


def iota(shape, axis):
    return lax.broadcasted_iota(I32, shape, axis)


def row_places(partner, me, n):
    rows = partner.shape[0]
    half = rows // n // 2
    own = (n + 1) * half
    local = partner % (n * rows)
    block, within = local // rows, local % rows
    index = jnp.arange(rows, dtype=I32)
    key = jnp.where(block < me, within, index)
    before = (block[None, :] == block[:, None]) & (key[None, :] < key[:, None])
    rank = jnp.sum(before.astype(I32), axis=1)
    shift = (block - me + n) % n
    owned = jnp.where(me < block, rank < half, rank >= half)
    step = (shift - 1) * half + rank % half
    place = jnp.where(block == me, rank, jnp.where(owned, 2 * half + step, own + step))
    found = jnp.sum(jnp.where(index[None, :] == within[:, None], place[None, :], 0), axis=1)
    mirror = jnp.where(block == me, rows + found, -1)
    return place, mirror


def gather_kernel(n, mine_ref, all_ref, landed, send_sem, recv_sem):
    me = lax.axis_index("col")
    barrier = pltpu.get_barrier_semaphore()
    for d in range(1, n):
        pl.semaphore_signal(barrier, inc=1, device_id={"col": lax.rem(me + d, n)}, device_id_type=MESH)
    pl.semaphore_wait(barrier, n - 1)

    def copy(d):
        return pltpu.make_async_remote_copy(
            src_ref=mine_ref, dst_ref=landed.at[d], send_sem=send_sem.at[d], recv_sem=recv_sem.at[d],
            device_id={"col": lax.rem(me + d, n)}, device_id_type=MESH,
        )

    for d in range(1, n):
        copy(d).start()
    all_ref[me] = mine_ref[...]
    for d in range(1, n):
        copy(d).wait_recv()
        all_ref[lax.rem(me + n - d, n)] = landed[d]
    for d in range(1, n):
        copy(d).wait_send()


def sort_kernel(n, half, occ, bc, slot_ref, count_ref, *refs):
    tiles, (place_ref, u_ref, w_ref, swap_ref) = refs[:bc], refs[bc:]
    i = pl.program_id(0)
    rows = place_ref.shape[2]
    tile = tiles[0].shape[3]
    own = (n + 1) * half

    total = swap_ref.shape[1]
    chunk = swap_ref.shape[0]
    x = iota((chunk, total), 0) + i * chunk
    y = iota((chunk, total), 1)
    swap_ref[...] = (x == (y % occ) * occ + y // occ).astype(F32).astype(BF16)

    for j in range(tile // rows):
        o = i * (tile // rows) + j
        equal = iota((rows, rows), 0) == place_ref[o]
        one_hot = equal.astype(F32).astype(BF16)
        for c in range(bc):
            live = (slot_ref[i * bc + c] < count_ref[0]).astype(F32).astype(BF16)
            part = tiles[c][0, 0, 0, j * rows : (j + 1) * rows, :] * live
            got = jnp.dot(one_hot, part, preferred_element_type=F32)
            at = slice(c * tile, (c + 1) * tile)
            u_ref[j, :, at] = got[:own].astype(BF16)
            for d in range(1, n):
                a = lax.rem(o + d, n)
                start = (n - d - 1) * half
                w_ref[a, start : start + half, at] = got[own + (d - 1) * half : own + d * half].astype(BF16)


def reduce_kernel(
    n, half, ranks, wide, u_hbm, w_hbm, swap_hbm, *refs
):
    held = ranks // 2 + 1
    given, refs = refs[:held], refs[held:]
    pieces = [given[0], given[1]]
    for piece in given[2:]:
        pieces += [piece, None]
    (
        z_ref, ubuf, wbuf, tall, t2buf, swap, sbuf, q1s, s1s, q1r, s1r, q2s, s2s, q2r, s2r, xqs, xss, xqr, xsr,
        usem, wsem, tsem, psem, q1a, q1b, s1a, s1b, q2a, q2b, s2a, s2b, xqa, xqb, xsa, xsb, psend, precv,
    ) = refs
    me = lax.axis_index("col")
    row = lax.axis_index("row")
    levels = n // 2
    level, side = me // 2, lax.rem(me, 2)
    other = me + 1 - 2 * side
    bc, tile, width = tall.shape
    depth = bc * tile
    share = tile // ranks
    own = (n + 1) * half
    chunks = n + 1

    def load_t(k):
        source = lax.rem(row + 2 * (k // 2), ranks)
        source = source if k % 2 == 0 else source + 1 - 2 * lax.rem(source, 2)
        first = pl.multiple_of(source * share, share)
        return pltpu.make_async_copy(pieces[k], tall.at[:, pl.ds(first, share), :], tsem.at[k])

    def swap_t(k):
        first = pl.multiple_of(lax.rem(row + 2 * (k // 2), ranks) * share, share)
        return pltpu.make_async_remote_copy(
            src_ref=pieces[k], dst_ref=tall.at[:, pl.ds(first, share), :], send_sem=psend.at[k], recv_sem=precv.at[k],
            device_id={"row": row + 1 - 2 * lax.rem(row, 2)}, device_id_type=MESH,
        )

    local = [k for k in range(ranks) if pieces[k] is not None]
    crossed = [k - 1 for k in range(ranks) if pieces[k] is None]
    load_p = pltpu.make_async_copy(swap_hbm, swap, psem)
    for k in local:
        load_t(k).start()
    load_p.start()

    def load(a):
        return (
            pltpu.make_async_copy(u_hbm.at[a], ubuf.at[a], usem.at[a]),
            pltpu.make_async_copy(w_hbm.at[a], wbuf.at[a], wsem.at[a]),
        )

    def owner(k, of_side):
        return 2 * lax.rem(level + 1 + k, levels) + of_side

    for copy in load(owner(0, 1 - side)):
        copy.start()

    barrier = pltpu.get_barrier_semaphore()
    for d in range(1, n):
        pl.semaphore_signal(barrier, inc=1, device_id={"col": lax.rem(me + d, n)}, device_id_type=MESH)
    pl.semaphore_signal(barrier, inc=1, device_id={"row": row + 1 - 2 * lax.rem(row, 2)}, device_id_type=MESH)
    pl.semaphore_wait(barrier, n)

    for k in crossed:
        swap_t(k).start()
    for k in local:
        load_t(k).wait()
    load_p.wait()
    for k in range(1, levels):
        for copy in load(owner(k, 1 - side)):
            copy.start()
    for k in range(levels):
        for copy in load(owner(k, side)):
            copy.start()
    for k in crossed:
        swap_t(k).wait_recv()
    high = 256
    per = tile // high
    parts = width // wide

    def columns(c):
        return pl.ds(pl.multiple_of(c * wide, wide), wide)

    def product(a, c, out, out_at):
        at = columns(c)
        first = jnp.dot(ubuf[a], tall[:, :, at].reshape(depth, wide), preferred_element_type=F32)
        second = jnp.dot(wbuf[a], t2buf[:, at], preferred_element_type=F32)
        out[0 : 2 * half, out_at] = first[: 2 * half]
        out[2 * half : own, out_at] = first[2 * half :] + second

    def remote(source, target, sent, arrived, device):
        return pltpu.make_async_remote_copy(
            src_ref=source, dst_ref=target, send_sem=sent, recv_sem=arrived,
            device_id={"col": device}, device_id_type=MESH,
        )

    def first_copy(c, k):
        u = c * levels + k
        return (
            remote(q1s.at[u], q1r.at[u], q1a.at[u], q1b.at[u], other),
            remote(s1s.at[u], s1r.at[u], s1a.at[u], s1b.at[u], other),
        )

    def second_copy(c, k):
        device = owner(k, side)
        u = c * levels + k
        return (
            remote(q2s.at[u], q2r.at[u], q2a.at[u], q2b.at[u], device),
            remote(s2s.at[u], s2r.at[u], s2a.at[u], s2b.at[u], device),
        )

    def last_copy(c, d):
        device = lax.rem(me + d, n)
        u, v = c * n + d, c * n + n - d
        return (
            remote(xqs.at[u], xqr.at[v], xqa.at[u], xqb.at[v], device),
            remote(xss.at[u], xsr.at[v], xsa.at[u], xsb.at[v], device),
        )

    group = 128 // half
    lane, line = iota((half, 128), 1), iota((half, 128), 0)

    def to_levels(part, m):
        most = jnp.max(jnp.abs(part), axis=1, keepdims=True)
        inverse = jnp.where(most > 1e-30, LEVELS / jnp.maximum(most, 1e-30), 0.0)
        here = lane == line + (m % group) * half
        scale = jnp.sum(jnp.where(here, most * (1.0 / LEVELS), 0.0), axis=0, keepdims=True)
        return jnp.round(part * inverse).astype(I32).astype(I16), scale

    def from_levels(value, scale, m):
        here = lane == line + (m % group) * half
        return value.astype(I32).astype(F32) * jnp.sum(jnp.where(here, scale, 0.0), axis=1, keepdims=True)

    def pack(u, value, q, s):
        for g in range(0, chunks, group):
            line_of = None
            for m in range(g, min(g + group, chunks)):
                q[u, m], scale = to_levels(value(m), m)
                line_of = scale if line_of is None else line_of + scale
            s[u, g // group : g // group + 1, :] = line_of

    def unpack(u, m, q, s):
        return from_levels(q[u, m], s[u, m // group : m // group + 1, :], m)

    def rows_of(m):
        return slice(m * half, (m + 1) * half)

    @pl.loop(0, parts + 2)
    def _(turn):
        @pl.when(turn < parts)
        def _():
            at = columns(turn)

            @pl.loop(0, depth // high)
            def _(k):
                source = tall.at[k // per, pl.ds(pl.multiple_of(lax.rem(k, per) * high, high), high), :]
                t2buf[pl.ds(pl.multiple_of(k * high, high), high), at] = jnp.dot(
                    source[...], swap[:, at], preferred_element_type=F32
                ).astype(BF16)

            @pl.loop(0, levels)
            def _(k):
                @pl.when(turn == 0)
                def _():
                    for copy in load(owner(k, 1 - side)):
                        copy.wait()

                product(owner(k, 1 - side), turn, sbuf, slice(None))
                pack(turn * levels + k, lambda m: sbuf[rows_of(m), :], q1s, s1s)
                for copy in first_copy(turn, k):
                    copy.start()

        @pl.when((turn >= 1) & (turn <= parts))
        def _():
            c = turn - 1

            @pl.loop(0, levels - 1)
            def _(k):
                @pl.when(c == 0)
                def _():
                    for copy in load(owner(k, side)):
                        copy.wait()

                product(owner(k, side), c, sbuf, slice(None))
                for copy in first_copy(c, k):
                    copy.wait_recv()
                u = c * levels + k
                pack(u, lambda m: sbuf[rows_of(m), :] + unpack(u, m, q1r, s1r), q2s, s2s)
                for copy in second_copy(c, k):
                    copy.start()

        @pl.when(turn >= 2)
        def _():
            c = turn - 2

            @pl.when(c == 0)
            def _():
                for copy in load(me):
                    copy.wait()

            at = columns(c)
            product(me, c, z_ref, at)

            def take(k, q, s):
                for m in range(chunks):
                    z_ref[rows_of(m), at] += unpack(c * levels + k, m, q, s)

            for copy in first_copy(c, levels - 1):
                copy.wait_recv()
            take(levels - 1, q1r, s1r)

            @pl.loop(0, levels - 1)
            def _(k):
                for copy in second_copy(c, k):
                    copy.wait_recv()
                take(k, q2r, s2r)

            for d in range(1, n):
                xqs[c * n + d], xss[c * n + d] = to_levels(z_ref[rows_of(d + 1), at], 0)
                for copy in last_copy(c, d):
                    copy.start()

    @pl.loop(0, parts)
    def _(c):
        for d in range(1, n):
            for copy in last_copy(c, d):
                copy.wait_recv()
            v = n - d
            z_ref[own + (v - 1) * half : own + v * half, columns(c)] = from_levels(xqr[c * n + v], xsr[c * n + v], 0)

    for k in crossed:
        swap_t(k).wait_send()

    @pl.loop(0, parts)
    def _(c):
        for d in range(1, n):
            for copy in last_copy(c, d):
                copy.wait_send()

        @pl.loop(0, levels)
        def _(k):
            for copy in first_copy(c, k):
                copy.wait_send()

        @pl.loop(0, levels - 1)
        def _(k):
            for copy in second_copy(c, k):
                copy.wait_send()


def final_kernel(
    half, own, z_ref, swap_ref, place_ref, mirror_ref, pair_ref, occ_ref, out_ref, pieces, hot_own, hot_far, hot_self, pair_of
):
    rows, width = z_ref.shape

    @pl.when(pl.program_id(0) == 0)
    def _():
        rest = z_ref[...]
        for p in range(2):
            piece = rest.astype(BF16)
            pieces[p] = piece
            rest = rest - piece.astype(F32)

        same = iota((rows, rows), 0) == iota((rows, rows), 1)

        def column(row):
            return jnp.sum(jnp.where(same, row, 0.0), axis=1, keepdims=True)

        place = column(place_ref[...].astype(F32)).astype(I32)
        mirror = column(mirror_ref[...].astype(F32)).astype(I32)
        pair_of[...] = jnp.broadcast_to(column(pair_ref[...]), pair_of.shape)

        def hot(out, first):
            number = iota(out.shape, 1) + first
            out[...] = ((number == place) | (number == mirror)).astype(F32).astype(BF16)

        hot(hot_own, 0)
        hot(hot_far, own)
        hot(hot_self, rows)

    chunk = out_ref.shape[1]
    at = pl.ds(pl.multiple_of(pl.program_id(0) * chunk, chunk), chunk)
    mixer = swap_ref[...]
    total = None
    for p in (1, 0):
        far = jnp.dot(pieces[p, own:, :], mixer, preferred_element_type=F32).astype(BF16)
        near = jnp.dot(pieces[p, : 2 * half, :], mixer, preferred_element_type=F32).astype(BF16)
        term = jnp.dot(hot_own[...], pieces[p, :own, at], preferred_element_type=F32)
        mine = jnp.dot(hot_self[...], near, preferred_element_type=F32)
        other = jnp.dot(hot_far[...], far, preferred_element_type=F32)
        term = term + (mine + other)
        total = term if total is None else total + term
    out_ref[...] = total / (pair_of[:, :1] - occ_ref[...])


def body(integrals, tile_count, tile_list, amplitudes, pair_energy, occ_energy, partner):
    n = lax.axis_size("col")
    me = lax.axis_index("col")
    rows = partner.shape[0]
    half = rows // n // 2
    own = (n + 1) * half
    slots, tile = integrals.shape[2], integrals.shape[3]
    bc, _, width = amplitudes.shape
    br = slots // bc
    occ = occ_energy.shape[0]
    depth = bc * tile

    place, mirror = row_places(partner, me, n)
    ranks = lax.axis_size("row")
    pieces = [amplitudes, lax.ppermute(amplitudes, "row", [(r ^ 1, r) for r in range(ranks)])]
    for k in range(2, ranks, 2):
        pieces.append(lax.ppermute(amplitudes, "row", [((r + k) % ranks, r) for r in range(ranks)]))

    dma = pltpu.SemaphoreType.DMA
    places = pl.pallas_call(
        functools.partial(gather_kernel, n),
        out_shape=jax.ShapeDtypeStruct((n, 1, rows), I32),
        in_specs=[pl.BlockSpec(memory_space=pltpu.VMEM)],
        out_specs=pl.BlockSpec(memory_space=pltpu.VMEM),
        scratch_shapes=[pltpu.VMEM((n, 1, rows), I32), dma((n,)), dma((n,))],
        compiler_params=pltpu.CompilerParams(collective_id=1, has_side_effects=True),
        name="gather_places",
    )(place[None, :])

    number = jnp.arange(slots, dtype=I32)
    slot = jnp.sum(jnp.where(tile_list[0, 0][None, :] == number[:, None], number[None, :], 0), axis=1)

    per = tile // rows

    def tile_spec(c):
        return pl.BlockSpec((1, 1, 1, tile, tile), lambda i, s, l: (0, 0, s[i * bc + c], 0, 0))

    u, w, swap = pl.pallas_call(
        functools.partial(sort_kernel, n, half, occ, bc),
        grid_spec=pltpu.PrefetchScalarGridSpec(
            num_scalar_prefetch=2,
            grid=(br,),
            in_specs=[tile_spec(c) for c in range(bc)] + [pl.BlockSpec((n, 1, rows), lambda i, s, l: (0, 0, 0))],
            out_specs=[
                pl.BlockSpec((per, own, depth), lambda i, s, l: (i, 0, 0)),
                pl.BlockSpec((n, rows - own, depth), lambda i, s, l: (0, 0, 0)),
                pl.BlockSpec((width // br, width), lambda i, s, l: (i, 0)),
            ],
        ),
        out_shape=[
            jax.ShapeDtypeStruct((n, own, depth), BF16),
            jax.ShapeDtypeStruct((n, rows - own, depth), BF16),
            jax.ShapeDtypeStruct((width, width), BF16),
        ],
        compiler_params=pltpu.CompilerParams(vmem_limit_bytes=63 * 1024 * 1024),
        cost_estimate=pl.CostEstimate(
            flops=2 * slots * rows * tile * tile, bytes_accessed=4 * slots * tile * tile, transcendentals=0
        ),
        name="sort_rows",
    )(slot, tile_count.reshape(1), *([integrals] * bc), places)

    anywhere = pl.BlockSpec(memory_space=pl.ANY)
    wide = 256
    parts = width // wide
    scale_rows = -(-(n + 1) // (128 // half))
    units = parts * (n // 2)
    packed = [pltpu.VMEM((units, n + 1, half, wide), I16), pltpu.VMEM((units, scale_rows, 128), F32)]
    last = [pltpu.VMEM((parts * n, half, wide), I16), pltpu.VMEM((parts * n, 1, 128), F32)]
    z = pl.pallas_call(
        functools.partial(reduce_kernel, n, half, ranks, wide),
        out_shape=jax.ShapeDtypeStruct((rows, width), F32),
        in_specs=[anywhere] * (3 + len(pieces)),
        out_specs=pl.BlockSpec(memory_space=pltpu.VMEM),
        scratch_shapes=[
            pltpu.VMEM((n, own, depth), BF16),
            pltpu.VMEM((n, rows - own, depth), BF16),
            pltpu.VMEM((bc, tile, width), BF16),
            pltpu.VMEM((depth, width), BF16),
            pltpu.VMEM((width, width), BF16),
            pltpu.VMEM((own, wide), F32),
            *(packed * 4),
            *(last * 2),
            dma((n,)), dma((n,)), dma((ranks,)), dma,
            *([dma((units,))] * 8),
            *([dma((parts * n,))] * 4),
            dma((ranks,)), dma((ranks,)),
        ],
        compiler_params=pltpu.CompilerParams(
            collective_id=0, has_side_effects=True, vmem_limit_bytes=63 * 1024 * 1024
        ),
        name="reduce_pairs",
    )(u, w, swap, *pieces)

    chunk = 256
    whole = lambda k: (0, 0)
    return pl.pallas_call(
        functools.partial(final_kernel, half, own),
        grid=(width // chunk,),
        in_specs=[
            pl.BlockSpec((rows, width), whole),
            pl.BlockSpec((width, chunk), lambda k: (0, k)),
            pl.BlockSpec((1, rows), whole),
            pl.BlockSpec((1, rows), whole),
            pl.BlockSpec((1, rows), whole),
            pl.BlockSpec((1, chunk), lambda k: (0, k)),
        ],
        out_specs=pl.BlockSpec((rows, chunk), lambda k: (0, k)),
        out_shape=jax.ShapeDtypeStruct((rows, width), F32),
        scratch_shapes=[
            pltpu.VMEM((2, rows, width), BF16),
            pltpu.VMEM((rows, own), BF16),
            pltpu.VMEM((rows, rows - own), BF16),
            pltpu.VMEM((rows, 2 * half), BF16),
            pltpu.VMEM((rows, 128), F32),
        ],
        compiler_params=pltpu.CompilerParams(vmem_limit_bytes=63 * 1024 * 1024),
        name="finish_rows",
    )(
        z, swap, place[None, :], mirror[None, :], pair_energy[None, :],
        (occ_energy[:, None] + occ_energy[None, :]).reshape(1, width),
    )


def solution(mesh):
    return jax.shard_map(
        body,
        mesh=mesh,
        in_specs=(
            P("row", "col", None, None, None),
            P("row", "col"),
            P("row", "col", None),
            P("col", "row", None),
            P(("row", "col")),
            P(),
            P(("row", "col")),
        ),
        out_specs=P(("row", "col"), None),
        check_vma=False,
    )
```
